512 devices in a mesh: seq: 64 (over y, z), tp: 8 (over x, core).
Axes of the slice: x: 4, y: 8, z: 8, core: 2. Of those that a mesh axis runs over, the one named last changes fastest.
Arguments:
- teacher_rows: bfloat16 [30720, 8192], P('seq', 'tp'), may hold values from -2700 to 2700, as said below
- teacher_gain: float32 [8192], P('tp'), may hold values from 0.1 to 1.9
- teacher_counts: int32 [64], replicated, may hold values from 288 to 480, as said below
- projector: bfloat16 [8192, 4096], P('tp', 'seq'), may hold values from -0.0625 to 0.0625
- student_rows: bfloat16 [24576, 4096], P('seq', 'tp'), may hold values from -2700 to 2700
- student_gain: float32 [4096], P('tp'), may hold values from 0.1 to 1.9
- span_shift: int32 [192], P('seq'), may hold values from -128 to 128, as said below
- span_len: int32 [192], P('seq'), may hold values from 64 to 128
- align_weights: bfloat16 [24576, 128], P('seq'), may hold values from 0.0099487305 to 1
Outputs:
- row_grad: bfloat16 [24576, 4096], P('seq', 'tp')
- gain_grad: float32 [4096], P('tp')
The draws below stay inside these ranges and needn't reach their ends.
Inputs may be any that keep to these rules, and one draw needn't show every extreme that they name: `teacher_counts`: the counts of indices 2m and 2m + 1 add up to 768; one index holds exactly 480 rows in every draw. `teacher_rows`: slots at or beyond an index's count hold no part of the sequence. `span_shift`: for the first block of each index of seq (k = 0) the shift lies in -128 .. -64; for the last (k = 2) it is 128.
All inputs are finite; a program needn't handle non-finite values.
Results may differ from the reference program's by a relative error of at most 0.014.
Values may be sent and summed in bfloat16 or wider, within the bound.
No kernel may reach another device: no remote copies, remote signals or barrier semaphores. Data moves between devices by JAX's collectives and lax.ppermute only.
A program may use at most 64 MiB of HBM per device.

```python
import math
import jax
import jax.numpy as jnp
from jax import lax

DT = 8192
DS = 4096
BLOCK = 128
BLK_DEV = 3
ROWS_DEV = 384
SPREAD = 96
JITTER = 128
TCAP = 480
SEQ_ROWS = 24576
BLOCKS = 192
N_SEQ = 64
N_TP = 8


def tilted_rows(key, row_count, width):
    keys = jax.random.split(key, 4)
    base_values = jnp.clip(jax.random.normal(keys[0], (row_count, width), jnp.float32), -6.0, 6.0)
    tilt = jax.random.uniform(keys[1], (row_count, 1), jnp.float32, 0.5, 1.5)
    column_place = jnp.arange(width, dtype=jnp.float32) / width
    roughness = jax.random.uniform(keys[2], (1, width), jnp.float32, 0.7, 1.4)
    row_scale = jnp.exp(jax.random.uniform(keys[3], (row_count, 1), jnp.float32, 0.0, 2.3))
    return base_values * jnp.exp(2.3 * tilt * column_place[None, :]) * roughness * row_scale


def draw_teacher_rows(key, part):
    return tilted_rows(jax.random.fold_in(key, 11), N_SEQ * TCAP, DT).astype(jnp.bfloat16)


def draw_student_rows(key, part):
    return tilted_rows(jax.random.fold_in(key, 23), ROWS_DEV * N_SEQ, DS).astype(jnp.bfloat16)


def draw_teacher_counts(key, part):
    keys = jax.random.split(jax.random.fold_in(key, 37), 2)
    half_count = N_SEQ // 2
    deviation = jax.random.randint(keys[0], (half_count,), 0 - SPREAD, SPREAD + 1)
    chosen = jax.random.randint(keys[1], (), 0, half_count)
    deviation = jnp.where(jnp.arange(half_count) == chosen, SPREAD, deviation)
    paired = jnp.stack([ROWS_DEV + deviation, ROWS_DEV - deviation], axis=1)
    return paired.reshape(N_SEQ).astype(jnp.int32)


def draw_span_shift(key, part):
    keys = jax.random.split(jax.random.fold_in(key, 53), 2)
    within = jnp.arange(BLK_DEV * N_SEQ, dtype=jnp.int32) % BLK_DEV
    general = jax.random.randint(keys[0], (BLK_DEV * N_SEQ,), 0 - JITTER, JITTER + 1)
    first = jax.random.randint(keys[1], (BLK_DEV * N_SEQ,), 0 - JITTER, 0 - JITTER // 2 + 1)
    last = jnp.full((BLK_DEV * N_SEQ,), JITTER, jnp.int32)
    shift = jnp.where(within == 0, first, jnp.where(within == BLK_DEV - 1, last, general))
    return shift.astype(jnp.int32)


def plant(array, own_key, least, largest):
    spot = [jax.random.randint(jax.random.fold_in(own_key, axis), (), 0, length) for axis, length in enumerate(array.shape)]
    longest = array.shape.index(max(array.shape))
    beside = spot[:longest] + [(spot[longest] + 1) % array.shape[longest]] + spot[longest + 1:]
    return array.at[tuple(spot)].set(least).at[tuple(beside)].set(largest)


def levels(key, extent, cuts, low, top_value):
    factor_of, own = 1.0, jax.random.fold_in(key, 6)
    for dim, parts in cuts:
        draws = jnp.exp(jax.random.uniform(jax.random.fold_in(own, dim), (parts,), jnp.float32, low / len(cuts), top_value / len(cuts)))
        factor_of = factor_of * jnp.repeat(draws, extent[dim] // parts).reshape([-1 if axis == dim else 1 for axis in range(len(extent))])
    return factor_of


def centred(stream_key, dims, scale, limit, cuts=(), kind=jnp.bfloat16):
    entries = jax.random.normal(stream_key, dims, jnp.float32) * scale
    if len(cuts) > 0:
        entries = levels(stream_key, dims, cuts, -0.22, 0.18) * entries
    return jnp.clip(entries, min=-limit, max=limit).astype(kind)


def setup_inputs(seed: int = 0) -> dict:
    seeds = jax.random.split(jax.random.key(seed), 10)
    teacher_rows = draw_teacher_rows(jax.random.fold_in(seeds[9], 71), 0)
    teacher_gain = jnp.clip(1.0 + 0.18 * jax.random.normal(seeds[1], (DT,), jnp.float32), 0.1, 1.9)
    teacher_counts = draw_teacher_counts(jax.random.fold_in(seeds[9], 71), 0)
    projector = centred(seeds[3], (DT, DS), DT ** -0.5, 0.0625, ((0, 8), (1, 64)))
    student_rows = draw_student_rows(jax.random.fold_in(seeds[9], 71), 0)
    student_gain = jnp.clip(1.0 + 0.18 * jax.random.normal(seeds[5], (DS,), jnp.float32), 0.1, 1.9)
    span_shift = draw_span_shift(jax.random.fold_in(seeds[9], 71), 0)
    span_len = plant(jax.random.randint(seeds[7], (BLOCKS,), BLOCK // 2, BLOCK + 1), jax.random.fold_in(seeds[7], 1), BLOCK // 2, BLOCK).astype(jnp.int32)
    align_weights = jnp.clip(jnp.exp(math.log(1.0) - 4.61031033 * jax.random.uniform(seeds[8], (SEQ_ROWS, BLOCK), jnp.float32) ** levels(seeds[8], (SEQ_ROWS, BLOCK), ((0, 64),), -0.2, 0.2)), 0.0099487305, 1.0).astype(jnp.bfloat16)
    return {"teacher_rows": teacher_rows, "teacher_gain": teacher_gain, "teacher_counts": teacher_counts, "projector": projector, "student_rows": student_rows, "student_gain": student_gain, "span_shift": span_shift, "span_len": span_len, "align_weights": align_weights}


epsilon = 1e-06

def reference(teacher_rows, teacher_gain, teacher_counts, projector, student_rows, student_gain, span_shift, span_len, align_weights):
    seq_rows = ROWS_DEV * N_SEQ
    starts = (jnp.cumsum(teacher_counts) - teacher_counts).astype(jnp.int32)
    positions = jnp.arange(seq_rows, dtype=jnp.int32)
    owner_device = (lax.optimization_barrier(jnp.sum((positions[:, None] >= starts[None, :]).astype(jnp.int32), axis=1)) - 1).astype(jnp.int32)
    source = (owner_device * TCAP + positions - jnp.take(starts, owner_device)).astype(jnp.int32)
    teacher_seq = jnp.take(teacher_rows, source, axis=0).astype(jnp.float32)
    teacher_scale = lax.rsqrt(lax.optimization_barrier(jnp.sum(teacher_seq * teacher_seq, axis=1)) / DT + epsilon)
    teacher_normed = (teacher_seq * teacher_scale[:, None] * teacher_gain.astype(jnp.float32)[None, :]).astype(jnp.bfloat16)
    group_width = DT // N_TP

    def add_group(group_index, accumulated):
        left_part = lax.dynamic_slice_in_dim(teacher_normed, group_index * group_width, group_width, 1)
        right_part = lax.dynamic_slice_in_dim(projector, group_index * group_width, group_width, 0)
        partial_sum = jnp.dot(left_part, right_part, preferred_element_type=jnp.float32).astype(jnp.bfloat16)
        partial_sum = lax.optimization_barrier(partial_sum)
        return accumulated + partial_sum.astype(jnp.float32)
    mapped = lax.fori_loop(0, N_TP, add_group, jnp.zeros((seq_rows, DS), jnp.float32)).astype(jnp.bfloat16)
    block_ids = jnp.arange(BLK_DEV * N_SEQ, dtype=jnp.int32)
    device = (block_ids // BLK_DEV).astype(jnp.int32)
    within = (block_ids % BLK_DEV).astype(jnp.int32)
    block_count = jnp.take(teacher_counts, device)
    span_start = jnp.take(starts, device) + within * block_count // BLK_DEV + span_shift
    span_start = jnp.clip(span_start, 0, seq_rows - span_len).astype(jnp.int32)
    offsets = jnp.arange(BLOCK, dtype=jnp.int32)
    window_index = jnp.clip(span_start[:, None] + offsets[None, :], 0, seq_rows - 1).astype(jnp.int32)
    live_mask = offsets[None, :] < span_len[:, None]
    weights = align_weights.reshape(BLK_DEV * N_SEQ, BLOCK, BLOCK)
    weights = jnp.where(live_mask[:, None, :], weights, jnp.zeros_like(weights))

    def mix_block(block_args):
        block_weights, block_index = block_args
        window = jnp.take(mapped, block_index, axis=0)
        return jnp.dot(block_weights, window, preferred_element_type=jnp.float32)
    target = lax.map(mix_block, (weights, window_index)).reshape(seq_rows, DS)
    target_hat = target * lax.rsqrt(lax.optimization_barrier(jnp.sum(target * target, axis=1, keepdims=True)) / DS + epsilon)
    student = student_rows.astype(jnp.float32)
    student_scale = lax.rsqrt(lax.optimization_barrier(jnp.sum(student * student, axis=1, keepdims=True)) / DS + epsilon)
    student_hat = student * student_scale
    residual = student_hat * student_gain[None, :] - target_hat
    weighted = residual * student_gain[None, :]
    inner_mean = lax.optimization_barrier(jnp.sum(weighted * student_hat, axis=1, keepdims=True)) / DS
    row_grad = (student_scale * (weighted - student_hat * inner_mean)).astype(jnp.bfloat16)
    gain_grad = lax.optimization_barrier(jnp.sum(residual * student_hat, axis=0)) / seq_rows
    return (row_grad, gain_grad)
```

```python
import functools

import jax
import jax.numpy as jnp
from jax import lax
from jax.experimental import pallas as pl
from jax.experimental.pallas import tpu as pltpu
from jax.sharding import PartitionSpec as P


epsilon = 1e-06
LEFT = 128
RIGHT = 160
SIDE = 8
F32 = jnp.float32
BF16 = jnp.bfloat16


def sent_to_all(value, axis):
    copies = jnp.broadcast_to(value, (lax.axis_size(axis), *value.shape))
    return lax.all_to_all(copies, axis, split_axis=0, concat_axis=0, tiled=True)


def moved(value, place):
    pairs = []
    for y in range(SIDE):
        for z in range(SIDE):
            for t in range(SIDE):
                y2, z2, t2 = place(y, z, t)
                pairs.append(((y * SIDE + z) * SIDE + t, (y2 * SIDE + z2) * SIDE + t2))
    return lax.ppermute(value, ("seq", "tp"), pairs)


def along_tp(value, to):
    return lax.ppermute(value, "tp", [(t, to(t)) for t in range(SIDE)])


def mix_body(place_ref, rows_ref, sums_ref, gain_ref, weights_ref, out_ref, *, slots, width):
    blocks, block = place_ref.shape[1], weights_ref.shape[1]
    total = rows_ref.shape[0]
    sums = jnp.sum(sums_ref[...], axis=0)
    scale = lax.rsqrt(sums / width + epsilon)
    within = lax.broadcasted_iota(jnp.int32, (block, total), 0)
    spot = lax.broadcasted_iota(jnp.int32, (block, total), 1)
    gain = gain_ref[...]
    rows = rows_ref[...]
    for k in range(blocks):
        start, length, count = place_ref[0, k], place_ref[1, k], place_ref[2, k]
        place = within + start
        held = jnp.where(
            place < 0,
            place + (slots + LEFT),
            jnp.where(place < count, place, place - count + (slots + LEFT)),
        )
        chosen = jnp.where((spot == held) & (within < length), 1.0, 0.0).astype(BF16)
        weights = weights_ref[pl.ds(k * block, block), :]
        spread = jnp.dot(weights, chosen, preferred_element_type=F32)
        spread = (spread * scale).astype(BF16)
        mixed = jnp.dot(spread, rows, preferred_element_type=F32)
        out_ref[pl.ds(k * block, block), :] = (mixed * gain).astype(BF16)


def row_sums(ones, value):
    return lax.dot_general(
        ones, value, (((1,), (1,)), ((), ())), precision=lax.Precision.HIGHEST, preferred_element_type=F32
    )


def project_body(order_ref, *refs):
    count = SIDE
    mixed_refs, (map_ref, student_ref, gain_ref, target_ref, sums_ref) = refs[:count], refs[count:]
    step = pl.program_id(0)
    for i in range(count):

        @pl.when(step == i)
        def _(i=i):
            part = lax.dot_general(
                mixed_refs[i][...], map_ref[0], (((1,), (1,)), ((), ())), preferred_element_type=F32
            )
            if i == 0:
                target_ref[...] = part
            else:
                target_ref[...] += part

    @pl.when(step == count - 1)
    def _():
        target = target_ref[...]
        student = student_ref[...].astype(F32)
        gain = gain_ref[...]
        ones = jnp.ones((8, student.shape[1]), F32)
        scaled = student * gain
        sums_ref[0] = row_sums(ones, target * target)[0:1]
        sums_ref[1] = row_sums(ones, target * scaled)[0:1]
        sums_ref[2] = row_sums(ones, student * student)[0:1]
        sums_ref[3] = row_sums(ones, scaled * scaled)[0:1]


def finish_body(sums_ref, target_ref, student_ref, gain_ref, grad_ref, terms_ref, *, width):
    total = jnp.sum(sums_ref[...], axis=0)
    total = jnp.concatenate([total[:, 0, :], jnp.zeros((4, total.shape[2]), F32)], axis=0)
    total = jnp.transpose(total)
    target_sums, cross, student_sums, gained = (total[:, k : k + 1] for k in range(4))
    target_scale = lax.rsqrt(target_sums / width + epsilon)
    student_scale = lax.rsqrt(student_sums / width + epsilon)
    inner = student_scale * (student_scale * gained - target_scale * cross) / width
    gain = gain_ref[...]
    student_hat = student_ref[...].astype(F32) * student_scale
    residual = student_hat * gain - target_ref[...] * target_scale
    grad_ref[...] = (student_scale * (residual * gain - student_hat * inner)).astype(BF16)
    terms_ref[...] = jnp.sum(residual * student_hat, axis=0, keepdims=True)


VMEM = pl.BlockSpec(memory_space=pltpu.VMEM)
SMEM = pl.BlockSpec(memory_space=pltpu.SMEM)


def shards(
    teacher_rows,
    teacher_gain,
    teacher_counts,
    projector,
    student_rows,
    student_gain,
    span_shift,
    span_len,
    align_weights,
):
    seq_count = lax.axis_size("seq")
    tp_count = lax.axis_size("tp")
    position = lax.axis_index("seq")
    tp_index = lax.axis_index("tp")
    slots, group = teacher_rows.shape
    teacher_width = group * tp_count
    rows_here, columns = student_rows.shape
    student_width = columns * tp_count
    blocks = span_shift.shape[0]
    seq_rows = rows_here * seq_count

    own_map = moved(projector.T, lambda y, z, t: (t, z, y))
    all_map = lax.all_gather(own_map, "seq", axis=0, tiled=True)
    all_map = all_map.reshape(SIDE, columns, group)

    own_count = jnp.take(teacher_counts, position)
    before = jnp.take(teacher_counts, jnp.maximum(position - 1, 0))
    own_start = jnp.where(position % 2 == 0, position * rows_here, (position - 1) * rows_here + before)
    last_rows = lax.dynamic_slice_in_dim(teacher_rows, own_count - LEFT, LEFT, axis=0)
    left = lax.ppermute(last_rows, "seq", [(i, (i + 1) % seq_count) for i in range(seq_count)])
    right = lax.ppermute(
        teacher_rows[:RIGHT], "seq", [(i, (i - 1) % seq_count) for i in range(seq_count)]
    )
    rows = jnp.concatenate([teacher_rows, left, right], axis=0)
    square_sums = sent_to_all(jnp.sum(jnp.square(rows.astype(F32)), axis=1)[None, :], "tp")
    block_ids = jnp.arange(blocks, dtype=jnp.int32)
    first = block_ids * own_count // blocks + span_shift
    first = jnp.clip(first, -own_start, seq_rows - span_len - own_start)
    place = jnp.stack([first, span_len, jnp.broadcast_to(own_count, (blocks,))]).astype(jnp.int32)
    mixed = pl.pallas_call(
        functools.partial(mix_body, slots=slots, width=teacher_width),
        out_shape=jax.ShapeDtypeStruct((rows_here, group), BF16),
        in_specs=[SMEM, VMEM, VMEM, VMEM, VMEM],
        out_specs=VMEM,
        name="mix",
    )(place, rows, square_sums, teacher_gain[None, :], align_weights)

    half = rows_here // 2
    up = along_tp(mixed, lambda t: (t + 2) % tp_count)
    down = along_tp(mixed, lambda t: (t - 2) % tp_count)
    far = jnp.concatenate(
        [
            along_tp(up[:half], lambda t: (t + 2) % tp_count),
            along_tp(down[half:], lambda t: (t - 2) % tp_count),
        ],
        axis=0,
    )
    parts = [mixed, up, down, far]
    parts += [along_tp(part, lambda t: t ^ 1) for part in parts]
    steps = jnp.array([0, -2, 2, 4], jnp.int32)
    order = jnp.concatenate([(tp_index + steps) % tp_count, ((tp_index ^ 1) + steps) % tp_count])

    whole = pl.BlockSpec((rows_here, group), lambda i, order: (0, 0))
    target, sums = pl.pallas_call(
        project_body,
        out_shape=(
            jax.ShapeDtypeStruct((rows_here, columns), F32),
            jax.ShapeDtypeStruct((4, 1, rows_here), F32),
        ),
        grid_spec=pltpu.PrefetchScalarGridSpec(
            num_scalar_prefetch=1,
            grid=(SIDE,),
            in_specs=[whole] * SIDE
            + [
                pl.BlockSpec((1, columns, group), lambda i, order: (order[i], 0, 0)),
                pl.BlockSpec((rows_here, columns), lambda i, order: (0, 0)),
                pl.BlockSpec((1, columns), lambda i, order: (0, 0)),
            ],
            out_specs=[
                pl.BlockSpec((rows_here, columns), lambda i, order: (0, 0)),
                pl.BlockSpec((4, 1, rows_here), lambda i, order: (0, 0, 0)),
            ],
        ),
        compiler_params=pltpu.CompilerParams(
            dimension_semantics=("arbitrary",), vmem_limit_bytes=48 << 20
        ),
        name="project",
    )(order.astype(jnp.int32), *parts, all_map, student_rows, student_gain[None, :])

    row_grad, terms = pl.pallas_call(
        functools.partial(finish_body, width=student_width),
        out_shape=(
            jax.ShapeDtypeStruct((rows_here, columns), BF16),
            jax.ShapeDtypeStruct((1, columns), F32),
        ),
        in_specs=[VMEM] * 4,
        out_specs=[VMEM] * 2,
        name="finish",
    )(sent_to_all(sums, "tp").reshape(tp_count, 4, 1, rows_here), target, student_rows, student_gain[None, :])
    gain_grad = sent_to_all(terms, "seq").sum(axis=(0, 1)) / seq_rows
    return (row_grad, gain_grad)


def solution(mesh):
    placed = (
        P("seq", "tp"),
        P("tp"),
        P(),
        P("tp", "seq"),
        P("seq", "tp"),
        P("tp"),
        P("seq"),
        P("seq"),
        P("seq", None),
    )
    return jax.shard_map(
        shards, mesh=mesh, in_specs=placed, out_specs=(P("seq", "tp"), P("tp")), check_vma=False
    )
```

```python
import functools

import jax
import jax.numpy as jnp
from jax import lax
from jax.experimental import pallas as pl
from jax.experimental.pallas import tpu as pltpu
from jax.sharding import PartitionSpec as P


epsilon = 1e-06
LEFT = 128
RIGHT = 160
SIDE = 8
F32 = jnp.float32
BF16 = jnp.bfloat16
VMEM = pl.BlockSpec(memory_space=pltpu.VMEM)
SMEM = pl.BlockSpec(memory_space=pltpu.SMEM)
HBM = pl.BlockSpec(memory_space=pltpu.HBM)
LANES = 128


def exchanged(copies, axis):
    return lax.all_to_all(copies, axis, split_axis=0, concat_axis=0, tiled=True)


def sent_to_all(value, axis):
    return exchanged(jnp.broadcast_to(value, (lax.axis_size(axis), *value.shape)), axis)


def moved(value, place):
    pairs = []
    for y in range(SIDE):
        for z in range(SIDE):
            for t in range(SIDE):
                y2, z2, t2 = place(y, z, t)
                pairs.append(((y * SIDE + z) * SIDE + t, (y2 * SIDE + z2) * SIDE + t2))
    return lax.ppermute(value, ("seq", "tp"), pairs)


def along_tp(value, to):
    return lax.ppermute(value, "tp", [(t, to(t)) for t in range(SIDE)])


def column(row):
    return jnp.transpose(jnp.broadcast_to(row, (128, row.shape[1])))[:, :1]


def row(values):
    return jnp.transpose(jnp.broadcast_to(values, (values.shape[0], 128)))[:1, :]


def times(left, right):
    return lax.dot_general(left, right, (((1,), (1,)), ((), ())), preferred_element_type=F32)


def student_body(student_ref, gain_ref, turned_ref, gained_ref, sums_ref):
    turned = jnp.transpose(student_ref[...].astype(F32))
    turned_ref[...] = turned.astype(BF16)
    sums_ref[0:1, :] = jnp.sum(turned * turned, axis=0, keepdims=True)
    gained = turned * column(gain_ref[...])
    gained_ref[...] = gained
    sums_ref[1:2, :] = jnp.sum(gained * gained, axis=0, keepdims=True)


def mix_body(place_ref, rows_ref, sums_ref, gain_ref, weights_ref, out_ref, *, slots, width):
    blocks, block = place_ref.shape[1], weights_ref.shape[1]
    total = rows_ref.shape[0]
    sums = jnp.sum(sums_ref[...], axis=0)[:, :total]
    scale = lax.rsqrt(sums / width + epsilon)
    within = lax.broadcasted_iota(jnp.int32, (block, total), 0)
    spot = lax.broadcasted_iota(jnp.int32, (block, total), 1)
    gain = gain_ref[...]
    rows = rows_ref[...]
    for k in range(blocks):
        start, length, count = place_ref[0, k], place_ref[1, k], place_ref[2, k]
        place = within + start
        held = jnp.where(
            place < 0,
            place + (slots + LEFT),
            jnp.where(place < count, place, place - count + (slots + LEFT)),
        )
        chosen = jnp.where((spot == held) & (within < length), 1.0, 0.0).astype(BF16)
        weights = weights_ref[pl.ds(k * block, block), :]
        spread = jnp.dot(weights, chosen, preferred_element_type=F32)
        spread = (spread * scale).astype(BF16)
        mixed = jnp.dot(spread, rows, preferred_element_type=F32)
        out_ref[pl.ds(k * block, block), :] = (mixed * gain).astype(BF16)


def ready_body(sums_ref, student_ref, gain_ref, rows_ref, base_ref, *, width):
    count = student_ref.shape[1]
    total = jnp.sum(sums_ref[...], axis=0)
    at = total.shape[1] - 2 * count
    student_scale = lax.rsqrt(total[:, at : at + count] / width + epsilon)
    rows_ref[0:1, :] = student_scale
    rows_ref[1:2, :] = student_scale * total[:, at + count :]
    student_hat = student_ref[...].astype(F32) * student_scale
    base_ref[...] = row(jnp.sum(student_hat * student_hat, axis=1, keepdims=True)) * gain_ref[...]


def project_body(order_ref, *refs):
    parts, refs = refs[:SIDE], refs[SIDE:]
    map_ref, gained_ref, _, target_out, sums_ref, total_ref, held, mixed, sem = refs
    near = SIDE - mixed.shape[0]
    copies = [[] for _ in range(SIDE)]
    for i in range(SIDE):
        copies[i].append(pltpu.make_async_copy(map_ref.at[order_ref[i]], held.at[i], sem.at[0, i]))
        if i >= near:
            copies[i].append(pltpu.make_async_copy(parts[i], mixed.at[i - near], sem.at[1, i]))
        for copy in copies[i]:
            copy.start()
    for i in range(SIDE):
        for copy in copies[i]:
            copy.wait()
        part = times(held[i], parts[i][...] if i < near else mixed[i - near])
        if i == 0:
            total_ref[...] = part
        else:
            total_ref[...] += part
    target = total_ref[...]
    target_out[...] = target.astype(BF16)
    sums_ref[:, 6:8, :] = jnp.zeros((SIDE, 2, LANES), F32)
    fill(sums_ref, 0, jnp.sum(target * target, axis=0, keepdims=True))
    fill(sums_ref, 3, jnp.sum(target * gained_ref[...], axis=0, keepdims=True))


def fill(ref, at, values):
    for k in range(values.shape[1] // LANES):
        piece = values[:, k * LANES : (k + 1) * LANES]
        ref[:, at + k : at + k + 1, :] = jnp.broadcast_to(piece[None], (ref.shape[0], 1, LANES))


def late_sums(sums_ref, width):
    total = jnp.sum(sums_ref[...], axis=0)
    target_sums = jnp.concatenate([total[k : k + 1] for k in range(3)], axis=1)
    cross = jnp.concatenate([total[k : k + 1] for k in range(3, 6)], axis=1)
    return lax.rsqrt(target_sums / width + epsilon), cross


def finish_body(sums_ref, rows_ref, base_ref, target_ref, student_ref, gain_ref, grad_ref, terms_ref, *, width):
    target_scale, cross = late_sums(sums_ref, width)
    scale = rows_ref[0:1, :]
    inner = scale * (rows_ref[1:2, :] - target_scale * cross) / width
    gain = column(gain_ref[...])
    student_hat = student_ref[...].astype(F32) * scale
    target_hat = target_ref[...].astype(F32) * target_scale
    taken = row(jnp.sum(target_hat * student_hat, axis=1, keepdims=True))
    fill(terms_ref, 0, base_ref[...] - taken)
    grad = scale * ((student_hat * gain - target_hat) * gain - student_hat * inner)
    grad_ref[...] = jnp.transpose(grad).astype(BF16)


def shards(
    teacher_rows,
    teacher_gain,
    teacher_counts,
    projector,
    student_rows,
    student_gain,
    span_shift,
    span_len,
    align_weights,
):
    seq_count = lax.axis_size("seq")
    tp_count = lax.axis_size("tp")
    position = lax.axis_index("seq")
    tp_index = lax.axis_index("tp")
    slots, group = teacher_rows.shape
    teacher_width = group * tp_count
    rows_here, columns = student_rows.shape
    student_width = columns * tp_count
    blocks = span_shift.shape[0]
    seq_rows = rows_here * seq_count
    gain_row = student_gain[None, :]

    own_map = moved(projector.T, lambda y, z, t: (t, z, y))

    own_count = jnp.take(teacher_counts, position)
    before = jnp.take(teacher_counts, jnp.maximum(position - 1, 0))
    own_start = jnp.where(position % 2 == 0, position * rows_here, (position - 1) * rows_here + before)
    last_rows = lax.dynamic_slice_in_dim(teacher_rows, own_count - LEFT, LEFT, axis=0)
    left = lax.ppermute(last_rows, "seq", [(i, (i + 1) % seq_count) for i in range(seq_count)])
    right = lax.ppermute(
        teacher_rows[:RIGHT], "seq", [(i, (i - 1) % seq_count) for i in range(seq_count)]
    )

    student, gained, student_sums = pl.pallas_call(
        student_body,
        out_shape=(
            jax.ShapeDtypeStruct((columns, rows_here), BF16),
            jax.ShapeDtypeStruct((columns, rows_here), F32),
            jax.ShapeDtypeStruct((2, rows_here), F32),
        ),
        in_specs=[VMEM] * 2,
        out_specs=[VMEM] * 3,
        name="student",
    )(student_rows, gain_row)

    all_map = lax.all_gather(own_map, "seq", axis=0, tiled=True).reshape(SIDE, columns, group)

    rows = jnp.concatenate([teacher_rows, left, right], axis=0)
    square_sums = jnp.sum(jnp.square(rows.astype(F32)), axis=1)
    early_sums = jnp.concatenate([square_sums, student_sums.reshape(-1)])[None, :]
    early_sums = sent_to_all(early_sums, "tp")
    block_ids = jnp.arange(blocks, dtype=jnp.int32)
    first = block_ids * own_count // blocks + span_shift
    first = jnp.clip(first, -own_start, seq_rows - span_len - own_start)
    place = jnp.stack([first, span_len, jnp.broadcast_to(own_count, (blocks,))]).astype(jnp.int32)
    mixed = pl.pallas_call(
        functools.partial(mix_body, slots=slots, width=teacher_width),
        out_shape=jax.ShapeDtypeStruct((rows_here, group), BF16),
        in_specs=[SMEM, VMEM, VMEM, VMEM, VMEM],
        out_specs=VMEM,
        name="mix",
    )(place, rows, early_sums, teacher_gain[None, :], align_weights)

    cut = rows_here // 2
    up = along_tp(mixed, lambda t: (t + 2) % tp_count)
    down = along_tp(mixed, lambda t: (t - 2) % tp_count)
    far = jnp.concatenate(
        [
            along_tp(up[:cut], lambda t: (t + 2) % tp_count),
            along_tp(down[cut:], lambda t: (t - 2) % tp_count),
        ],
        axis=0,
    )
    parts = [mixed, up, down, far]
    near = len(parts)
    parts += [along_tp(part, lambda t: t ^ 1) for part in parts]
    shifts = jnp.array([0, -2, 2, 4], jnp.int32)
    order = jnp.concatenate([(tp_index + shifts) % tp_count, ((tp_index ^ 1) + shifts) % tp_count])

    scale_rows, base = pl.pallas_call(
        functools.partial(ready_body, width=student_width),
        out_shape=(
            jax.ShapeDtypeStruct((2, rows_here), F32),
            jax.ShapeDtypeStruct((1, columns), F32),
        ),
        in_specs=[VMEM] * 3,
        out_specs=[VMEM] * 2,
        name="ready",
    )(early_sums, student, gain_row)

    target, sums = pl.pallas_call(
        project_body,
        out_shape=(
            jax.ShapeDtypeStruct((columns, rows_here), BF16),
            jax.ShapeDtypeStruct((tp_count, 8, LANES), F32),
        ),
        in_specs=[SMEM] + [VMEM] * near + [HBM] * (SIDE - near) + [HBM, VMEM, HBM],
        out_specs=[VMEM] * 2,
        scratch_shapes=[
            pltpu.VMEM((columns, rows_here), F32),
            pltpu.VMEM((SIDE, columns, group), BF16),
            pltpu.VMEM((SIDE - near, rows_here, group), BF16),
            pltpu.SemaphoreType.DMA((2, SIDE)),
        ],
        compiler_params=pltpu.CompilerParams(vmem_limit_bytes=50 << 20),
        name="project",
    )(order.astype(jnp.int32), *parts, all_map, gained, scale_rows)

    row_grad, terms = pl.pallas_call(
        functools.partial(finish_body, width=student_width),
        out_shape=(
            jax.ShapeDtypeStruct((rows_here, columns), BF16),
            jax.ShapeDtypeStruct((seq_count, columns // LANES, LANES), F32),
        ),
        in_specs=[VMEM] * 6,
        out_specs=[VMEM] * 2,
        name="finish",
    )(exchanged(sums, "tp"), scale_rows, base, target, student, gain_row)
    gain_grad = exchanged(terms, "seq").sum(axis=0).reshape(columns) / seq_rows
    return (row_grad, gain_grad)


def solution(mesh):
    placed = (
        P("seq", "tp"),
        P("tp"),
        P(),
        P("tp", "seq"),
        P("seq", "tp"),
        P("tp"),
        P("seq"),
        P("seq"),
        P("seq", None),
    )
    return jax.shard_map(
        shards, mesh=mesh, in_specs=placed, out_specs=(P("seq", "tp"), P("tp")), check_vma=False
    )
```

```python
import functools

import jax
import jax.numpy as jnp
from jax import lax
from jax.experimental import pallas as pl
from jax.experimental.pallas import tpu as pltpu
from jax.sharding import PartitionSpec as P


epsilon = 1e-06
LEFT = 128
RIGHT = 160
SIDE = 8
F32 = jnp.float32
BF16 = jnp.bfloat16
VMEM = pl.BlockSpec(memory_space=pltpu.VMEM)
SMEM = pl.BlockSpec(memory_space=pltpu.SMEM)
HBM = pl.BlockSpec(memory_space=pltpu.HBM)
LANES = 128


def exchanged(copies, axis):
    return lax.all_to_all(copies, axis, split_axis=0, concat_axis=0, tiled=True)


def sent_to_all(value, axis):
    return exchanged(jnp.broadcast_to(value, (lax.axis_size(axis), *value.shape)), axis)


def moved(value, place):
    pairs = []
    for y in range(SIDE):
        for z in range(SIDE):
            for t in range(SIDE):
                y2, z2, t2 = place(y, z, t)
                pairs.append(((y * SIDE + z) * SIDE + t, (y2 * SIDE + z2) * SIDE + t2))
    return lax.ppermute(value, ("seq", "tp"), pairs)


def along_tp(value, to):
    return lax.ppermute(value, "tp", [(t, to(t)) for t in range(SIDE)])


def column(row):
    return jnp.transpose(jnp.broadcast_to(row, (128, row.shape[1])))[:, :1]


def row(values):
    return jnp.transpose(jnp.broadcast_to(values, (values.shape[0], 128)))[:1, :]


def times(left, right):
    return lax.dot_general(left, right, (((1,), (1,)), ((), ())), preferred_element_type=F32)


def student_body(student_ref, gain_ref, turned_ref, gained_ref, sums_ref):
    turned = jnp.transpose(student_ref[...].astype(F32))
    turned_ref[...] = turned.astype(BF16)
    sums_ref[0:1, :] = jnp.sum(turned * turned, axis=0, keepdims=True)
    gained = turned * column(gain_ref[...])
    gained_ref[...] = gained
    sums_ref[1:2, :] = jnp.sum(gained * gained, axis=0, keepdims=True)


def mix_body(place_ref, rows_ref, sums_ref, gain_ref, weights_ref, out_ref, *, slots, width):
    blocks, block = place_ref.shape[1], weights_ref.shape[1]
    total = rows_ref.shape[0]
    sums = jnp.sum(sums_ref[...], axis=0)[:, :total]
    scale = lax.rsqrt(sums / width + epsilon)
    within = lax.broadcasted_iota(jnp.int32, (block, total), 0)
    spot = lax.broadcasted_iota(jnp.int32, (block, total), 1)
    gain = gain_ref[...]
    rows = rows_ref[...]
    for k in range(blocks):
        start, length, count = place_ref[0, k], place_ref[1, k], place_ref[2, k]
        place = within + start
        held = jnp.where(
            place < 0,
            place + (slots + LEFT),
            jnp.where(place < count, place, place - count + (slots + LEFT)),
        )
        chosen = jnp.where((spot == held) & (within < length), 1.0, 0.0).astype(BF16)
        weights = weights_ref[pl.ds(k * block, block), :]
        spread = jnp.dot(weights, chosen, preferred_element_type=F32)
        spread = (spread * scale).astype(BF16)
        mixed = jnp.dot(spread, rows, preferred_element_type=F32)
        out_ref[pl.ds(k * block, block), :] = (mixed * gain).astype(BF16)


def ready_body(sums_ref, student_ref, gain_ref, rows_ref, base_ref, *, width):
    count = student_ref.shape[1]
    total = jnp.sum(sums_ref[...], axis=0)
    at = total.shape[1] - 2 * count
    student_scale = lax.rsqrt(total[:, at : at + count] / width + epsilon)
    rows_ref[0:1, :] = student_scale
    rows_ref[1:2, :] = student_scale * total[:, at + count :]
    student_hat = student_ref[...].astype(F32) * student_scale
    base_ref[...] = row(jnp.sum(student_hat * student_hat, axis=1, keepdims=True)) * gain_ref[...]


def project_body(order_ref, *refs):
    parts, refs = refs[:SIDE], refs[SIDE:]
    map_ref, gained_in, target_out, sums_ref, total_ref, rounded_ref, gained_ref, held, mixed, sem, side_sem = refs
    near = SIDE - mixed.shape[0]
    copies = [[] for _ in range(SIDE)]
    for i in range(SIDE):
        copies[i].append(pltpu.make_async_copy(map_ref.at[order_ref[i]], held.at[i], sem.at[0, i]))
        if i >= near:
            copies[i].append(pltpu.make_async_copy(parts[i], mixed.at[i - near], sem.at[1, i]))
        for copy in copies[i]:
            copy.start()
    take_gained = pltpu.make_async_copy(gained_in, gained_ref, side_sem.at[0])
    take_gained.start()
    for i in range(SIDE):
        for copy in copies[i]:
            copy.wait()
        part = times(parts[i][...] if i < near else mixed[i - near], held[i])
        if i == 0:
            total_ref[...] = part
        else:
            total_ref[...] += part
    target = jnp.transpose(total_ref[...])
    rounded_ref[...] = target.astype(BF16)
    send = pltpu.make_async_copy(rounded_ref, target_out, side_sem.at[1])
    send.start()
    take_gained.wait()
    sums_ref[:, 6:8, :] = jnp.zeros((SIDE, 2, LANES), F32)
    fill(sums_ref, 0, jnp.sum(target * target, axis=0, keepdims=True))
    fill(sums_ref, 3, jnp.sum(target * gained_ref[...], axis=0, keepdims=True))
    send.wait()


def fill(ref, at, values):
    for k in range(values.shape[1] // LANES):
        piece = values[:, k * LANES : (k + 1) * LANES]
        ref[:, at + k : at + k + 1, :] = jnp.broadcast_to(piece[None], (ref.shape[0], 1, LANES))


def late_sums(sums_ref, width):
    total = jnp.sum(sums_ref[...], axis=0)
    target_sums = jnp.concatenate([total[k : k + 1] for k in range(3)], axis=1)
    cross = jnp.concatenate([total[k : k + 1] for k in range(3, 6)], axis=1)
    return lax.rsqrt(target_sums / width + epsilon), cross


def terms_body(sums_ref, rows_ref, base_ref, target_ref, student_ref, terms_ref, *, width):
    target_scale, _ = late_sums(sums_ref, width)
    scale = target_scale * rows_ref[0:1, :]
    cross = target_ref[...].astype(F32) * student_ref[...].astype(F32)
    taken = row(jnp.sum(cross * scale, axis=1, keepdims=True))
    fill(terms_ref, 0, base_ref[...] - taken)


def grad_body(sums_ref, rows_ref, target_ref, student_ref, gain_ref, grad_ref, *, width):
    target_scale, cross = late_sums(sums_ref, width)
    scale = rows_ref[0:1, :]
    inner = scale * (rows_ref[1:2, :] - target_scale * cross) / width
    gain = column(gain_ref[...])
    student_hat = student_ref[...].astype(F32) * scale
    target_hat = target_ref[...].astype(F32) * target_scale
    grad = scale * ((student_hat * gain - target_hat) * gain - student_hat * inner)
    grad_ref[...] = jnp.transpose(grad).astype(BF16)


def shards(
    teacher_rows,
    teacher_gain,
    teacher_counts,
    projector,
    student_rows,
    student_gain,
    span_shift,
    span_len,
    align_weights,
):
    seq_count = lax.axis_size("seq")
    tp_count = lax.axis_size("tp")
    position = lax.axis_index("seq")
    tp_index = lax.axis_index("tp")
    slots, group = teacher_rows.shape
    teacher_width = group * tp_count
    rows_here, columns = student_rows.shape
    student_width = columns * tp_count
    blocks = span_shift.shape[0]
    seq_rows = rows_here * seq_count
    gain_row = student_gain[None, :]

    own_map = moved(projector.T, lambda y, z, t: (t, z, y))

    own_count = jnp.take(teacher_counts, position)
    before = jnp.take(teacher_counts, jnp.maximum(position - 1, 0))
    own_start = jnp.where(position % 2 == 0, position * rows_here, (position - 1) * rows_here + before)
    last_rows = lax.dynamic_slice_in_dim(teacher_rows, own_count - LEFT, LEFT, axis=0)
    left = lax.ppermute(last_rows, "seq", [(i, (i + 1) % seq_count) for i in range(seq_count)])
    right = lax.ppermute(
        teacher_rows[:RIGHT], "seq", [(i, (i - 1) % seq_count) for i in range(seq_count)]
    )

    student, gained, student_sums = pl.pallas_call(
        student_body,
        out_shape=(
            jax.ShapeDtypeStruct((columns, rows_here), BF16),
            jax.ShapeDtypeStruct((columns, rows_here), F32),
            jax.ShapeDtypeStruct((2, rows_here), F32),
        ),
        in_specs=[VMEM] * 2,
        out_specs=[VMEM] * 3,
        name="student",
    )(student_rows, gain_row)

    all_map = lax.all_gather(own_map, "seq", axis=0, tiled=True).reshape(SIDE, columns, group)

    rows = jnp.concatenate([teacher_rows, left, right], axis=0)
    square_sums = jnp.sum(jnp.square(rows.astype(F32)), axis=1)
    early_sums = jnp.concatenate([square_sums, student_sums.reshape(-1)])[None, :]
    early_sums = sent_to_all(early_sums, "tp")
    scale_rows, base = pl.pallas_call(
        functools.partial(ready_body, width=student_width),
        out_shape=(
            jax.ShapeDtypeStruct((2, rows_here), F32),
            jax.ShapeDtypeStruct((1, columns), F32),
        ),
        in_specs=[VMEM] * 3,
        out_specs=[VMEM] * 2,
        name="ready",
    )(early_sums, student, gain_row)
    block_ids = jnp.arange(blocks, dtype=jnp.int32)
    first = block_ids * own_count // blocks + span_shift
    first = jnp.clip(first, -own_start, seq_rows - span_len - own_start)
    place = jnp.stack([first, span_len, jnp.broadcast_to(own_count, (blocks,))]).astype(jnp.int32)
    mixed = pl.pallas_call(
        functools.partial(mix_body, slots=slots, width=teacher_width),
        out_shape=jax.ShapeDtypeStruct((rows_here, group), BF16),
        in_specs=[SMEM, VMEM, VMEM, VMEM, VMEM],
        out_specs=VMEM,
        name="mix",
    )(place, rows, early_sums, teacher_gain[None, :], align_weights)

    mixed, scale_rows, base = lax.optimization_barrier((mixed, scale_rows, base))

    cut = rows_here // 2
    up = along_tp(mixed, lambda t: (t + 2) % tp_count)
    down = along_tp(mixed, lambda t: (t - 2) % tp_count)
    far = jnp.concatenate(
        [
            along_tp(up[:cut], lambda t: (t + 2) % tp_count),
            along_tp(down[cut:], lambda t: (t - 2) % tp_count),
        ],
        axis=0,
    )
    parts = [mixed, up, down, far]
    near = len(parts)
    parts += [along_tp(part, lambda t: t ^ 1) for part in parts]
    shifts = jnp.array([0, -2, 2, 4], jnp.int32)
    order = jnp.concatenate([(tp_index + shifts) % tp_count, ((tp_index ^ 1) + shifts) % tp_count])

    target, sums = pl.pallas_call(
        project_body,
        out_shape=(
            pltpu.HBM((columns, rows_here), BF16),
            jax.ShapeDtypeStruct((tp_count, 8, LANES), F32),
        ),
        in_specs=[SMEM] + [VMEM] * near + [HBM] * (SIDE - near + 2),
        out_specs=[HBM, VMEM],
        scratch_shapes=[
            pltpu.VMEM((rows_here, columns), F32),
            pltpu.VMEM((columns, rows_here), BF16),
            pltpu.VMEM((columns, rows_here), F32),
            pltpu.VMEM((SIDE, columns, group), BF16),
            pltpu.VMEM((SIDE - near, rows_here, group), BF16),
            pltpu.SemaphoreType.DMA((2, SIDE)),
            pltpu.SemaphoreType.DMA((2,)),
        ],
        compiler_params=pltpu.CompilerParams(vmem_limit_bytes=26 << 20),
        name="project",
    )(
        order.astype(jnp.int32),
        *parts,
        pltpu.with_memory_space_constraint(all_map, pltpu.HBM),
        pltpu.with_memory_space_constraint(gained, pltpu.HBM),
    )

    sums = exchanged(sums, "tp")
    terms = pl.pallas_call(
        functools.partial(terms_body, width=student_width),
        out_shape=jax.ShapeDtypeStruct((seq_count, columns // LANES, LANES), F32),
        in_specs=[VMEM] * 5,
        out_specs=VMEM,
        name="terms",
    )(sums, scale_rows, base, target, student)
    gain_grad = exchanged(terms, "seq").sum(axis=0).reshape(columns) / seq_rows
    row_grad = pl.pallas_call(
        functools.partial(grad_body, width=student_width),
        out_shape=jax.ShapeDtypeStruct((rows_here, columns), BF16),
        in_specs=[VMEM] * 5,
        out_specs=VMEM,
        cost_estimate=pl.CostEstimate(flops=4 << 20, bytes_accessed=2 << 20, transcendentals=0),
        name="grad",
    )(sums, scale_rows, target, student, gain_row)
    return (row_grad, gain_grad)


def solution(mesh):
    placed = (
        P("seq", "tp"),
        P("tp"),
        P(),
        P("tp", "seq"),
        P("seq", "tp"),
        P("tp"),
        P("seq"),
        P("seq"),
        P("seq", None),
    )
    return jax.shard_map(
        shards, mesh=mesh, in_specs=placed, out_specs=(P("seq", "tp"), P("tp")), check_vma=False
    )
```

```python
import functools

import jax
import jax.numpy as jnp
from jax import lax
from jax.experimental import pallas as pl
from jax.experimental.pallas import tpu as pltpu
from jax.sharding import PartitionSpec as P


epsilon = 1e-06
LEFT = 128
RIGHT = 160
SIDE = 8
F32 = jnp.float32
BF16 = jnp.bfloat16
VMEM = pl.BlockSpec(memory_space=pltpu.VMEM)
SMEM = pl.BlockSpec(memory_space=pltpu.SMEM)
HBM = pl.BlockSpec(memory_space=pltpu.HBM)
LANES = 128


def exchanged(copies, axis):
    return lax.all_to_all(copies, axis, split_axis=0, concat_axis=0, tiled=True)


def sent_to_all(value, axis):
    return exchanged(jnp.broadcast_to(value, (lax.axis_size(axis), *value.shape)), axis)


def moved(value, place):
    pairs = []
    for y in range(SIDE):
        for z in range(SIDE):
            for t in range(SIDE):
                y2, z2, t2 = place(y, z, t)
                pairs.append(((y * SIDE + z) * SIDE + t, (y2 * SIDE + z2) * SIDE + t2))
    return lax.ppermute(value, ("seq", "tp"), pairs)


def along_tp(value, to):
    return lax.ppermute(value, "tp", [(t, to(t)) for t in range(SIDE)])


def column(row):
    return jnp.transpose(jnp.broadcast_to(row, (128, row.shape[1])))[:, :1]


def row(values):
    return jnp.transpose(jnp.broadcast_to(values, (values.shape[0], 128)))[:1, :]


def times(left, right):
    return lax.dot_general(left, right, (((1,), (1,)), ((), ())), preferred_element_type=F32)


def student_body(student_ref, gain_ref, turned_ref, gained_ref, sums_ref):
    turned = jnp.transpose(student_ref[...].astype(F32))
    turned_ref[...] = turned.astype(BF16)
    sums_ref[0:1, :] = jnp.sum(turned * turned, axis=0, keepdims=True)
    gained = turned * column(gain_ref[...])
    gained_ref[...] = gained
    sums_ref[1:2, :] = jnp.sum(gained * gained, axis=0, keepdims=True)


def mix_body(place_ref, rows_ref, sums_ref, gain_ref, weights_ref, out_ref, *, slots, width):
    blocks, block = place_ref.shape[1], weights_ref.shape[1]
    total = rows_ref.shape[0]
    sums = jnp.sum(sums_ref[...], axis=0)[:, :total]
    scale = lax.rsqrt(sums / width + epsilon)
    within = lax.broadcasted_iota(jnp.int32, (block, total), 0)
    spot = lax.broadcasted_iota(jnp.int32, (block, total), 1)
    gain = gain_ref[...]
    rows = rows_ref[...]
    for k in range(blocks):
        start, length, count = place_ref[0, k], place_ref[1, k], place_ref[2, k]
        place = within + start
        held = jnp.where(
            place < 0,
            place + (slots + LEFT),
            jnp.where(place < count, place, place - count + (slots + LEFT)),
        )
        chosen = jnp.where((spot == held) & (within < length), 1.0, 0.0).astype(BF16)
        weights = weights_ref[pl.ds(k * block, block), :]
        spread = jnp.dot(weights, chosen, preferred_element_type=F32)
        spread = (spread * scale).astype(BF16)
        mixed = jnp.dot(spread, rows, preferred_element_type=F32)
        out_ref[pl.ds(k * block, block), :] = (mixed * gain).astype(BF16)


def ready_body(sums_ref, student_ref, gain_ref, rows_ref, base_ref, *, width):
    count = student_ref.shape[1]
    total = jnp.sum(sums_ref[...], axis=0)
    at = total.shape[1] - 2 * count
    student_scale = lax.rsqrt(total[:, at : at + count] / width + epsilon)
    rows_ref[0:1, :] = student_scale
    rows_ref[1:2, :] = student_scale * total[:, at + count :]
    student_hat = student_ref[...].astype(F32) * student_scale
    base_ref[...] = row(jnp.sum(student_hat * student_hat, axis=1, keepdims=True)) * gain_ref[...]


def project_body(order_ref, *refs):
    parts, refs = refs[:SIDE], refs[SIDE:]
    map_ref, gained_in, target_out, sums_ref, total_ref, rounded_ref, gained_ref, held, mixed, sem, side_sem = refs
    near = SIDE - mixed.shape[0]
    copies = [[] for _ in range(SIDE)]
    for i in range(SIDE):
        copies[i].append(pltpu.make_async_copy(map_ref.at[order_ref[i]], held.at[i], sem.at[0, i]))
        if i >= near:
            copies[i].append(pltpu.make_async_copy(parts[i], mixed.at[i - near], sem.at[1, i]))
        for copy in copies[i]:
            copy.start()
    take_gained = pltpu.make_async_copy(gained_in, gained_ref, side_sem.at[0])
    take_gained.start()
    for i in range(SIDE):
        for copy in copies[i]:
            copy.wait()
        part = times(parts[i][...] if i < near else mixed[i - near], held[i])
        if i == 0:
            total_ref[...] = part
        else:
            total_ref[...] += part
    target = jnp.transpose(total_ref[...])
    rounded_ref[...] = target.astype(BF16)
    send = pltpu.make_async_copy(rounded_ref, target_out, side_sem.at[1])
    send.start()
    take_gained.wait()
    sums_ref[:, 6:8, :] = jnp.zeros((SIDE, 2, LANES), F32)
    fill(sums_ref, 0, jnp.sum(target * target, axis=0, keepdims=True))
    fill(sums_ref, 3, jnp.sum(target * gained_ref[...], axis=0, keepdims=True))
    send.wait()


def fill(ref, at, values):
    for k in range(values.shape[1] // LANES):
        piece = values[:, k * LANES : (k + 1) * LANES]
        ref[:, at + k : at + k + 1, :] = jnp.broadcast_to(piece[None], (ref.shape[0], 1, LANES))


def late_sums(sums_ref, width):
    total = jnp.sum(sums_ref[...], axis=0)
    target_sums = jnp.concatenate([total[k : k + 1] for k in range(3)], axis=1)
    cross = jnp.concatenate([total[k : k + 1] for k in range(3, 6)], axis=1)
    return lax.rsqrt(target_sums / width + epsilon), cross


def terms_body(sums_ref, rows_ref, base_ref, target_ref, student_ref, terms_ref, *, width, count):
    target_scale, _ = late_sums(sums_ref, width)
    scale = target_scale * rows_ref[0:1, :]
    cross = target_ref[...].astype(F32) * student_ref[...].astype(F32)
    taken = row(jnp.sum(cross * scale, axis=1, keepdims=True))
    fill(terms_ref, 0, (base_ref[...] - taken) / count)


def grad_body(sums_ref, rows_ref, target_ref, student_ref, gain_ref, grad_ref, *, width):
    target_scale, cross = late_sums(sums_ref, width)
    scale = rows_ref[0:1, :]
    inner = scale * (rows_ref[1:2, :] - target_scale * cross) / width
    gain = column(gain_ref[...])
    student_hat = student_ref[...].astype(F32) * scale
    target_hat = target_ref[...].astype(F32) * target_scale
    grad = scale * ((student_hat * gain - target_hat) * gain - student_hat * inner)
    grad_ref[...] = jnp.transpose(grad).astype(BF16)


def shards(
    teacher_rows,
    teacher_gain,
    teacher_counts,
    projector,
    student_rows,
    student_gain,
    span_shift,
    span_len,
    align_weights,
):
    seq_count = lax.axis_size("seq")
    tp_count = lax.axis_size("tp")
    position = lax.axis_index("seq")
    tp_index = lax.axis_index("tp")
    slots, group = teacher_rows.shape
    teacher_width = group * tp_count
    rows_here, columns = student_rows.shape
    student_width = columns * tp_count
    blocks = span_shift.shape[0]
    seq_rows = rows_here * seq_count
    gain_row = student_gain[None, :]

    own_map = moved(projector.T, lambda y, z, t: (t, z, y))

    own_count = jnp.take(teacher_counts, position)
    before = jnp.take(teacher_counts, jnp.maximum(position - 1, 0))
    own_start = jnp.where(position % 2 == 0, position * rows_here, (position - 1) * rows_here + before)
    last_rows = lax.dynamic_slice_in_dim(teacher_rows, own_count - LEFT, LEFT, axis=0)
    left = lax.ppermute(last_rows, "seq", [(i, (i + 1) % seq_count) for i in range(seq_count)])
    right = lax.ppermute(
        teacher_rows[:RIGHT], "seq", [(i, (i - 1) % seq_count) for i in range(seq_count)]
    )

    student, gained, student_sums = pl.pallas_call(
        student_body,
        out_shape=(
            jax.ShapeDtypeStruct((columns, rows_here), BF16),
            jax.ShapeDtypeStruct((columns, rows_here), F32),
            jax.ShapeDtypeStruct((2, rows_here), F32),
        ),
        in_specs=[VMEM] * 2,
        out_specs=[VMEM] * 3,
        name="student",
    )(student_rows, gain_row)

    all_map = lax.all_gather(own_map, "seq", axis=0, tiled=True).reshape(SIDE, columns, group)

    rows = jnp.concatenate([teacher_rows, left, right], axis=0)
    square_sums = jnp.sum(jnp.square(rows.astype(F32)), axis=1)
    early_sums = jnp.concatenate([square_sums, student_sums.reshape(-1)])[None, :]
    early_sums = sent_to_all(early_sums, "tp")
    scale_rows, base = pl.pallas_call(
        functools.partial(ready_body, width=student_width),
        out_shape=(
            jax.ShapeDtypeStruct((2, rows_here), F32),
            jax.ShapeDtypeStruct((1, columns), F32),
        ),
        in_specs=[VMEM] * 3,
        out_specs=[VMEM] * 2,
        name="ready",
    )(early_sums, student, gain_row)
    block_ids = jnp.arange(blocks, dtype=jnp.int32)
    first = block_ids * own_count // blocks + span_shift
    first = jnp.clip(first, -own_start, seq_rows - span_len - own_start)
    place = jnp.stack([first, span_len, jnp.broadcast_to(own_count, (blocks,))]).astype(jnp.int32)
    mixed = pl.pallas_call(
        functools.partial(mix_body, slots=slots, width=teacher_width),
        out_shape=jax.ShapeDtypeStruct((rows_here, group), BF16),
        in_specs=[SMEM, VMEM, VMEM, VMEM, VMEM],
        out_specs=VMEM,
        name="mix",
    )(place, rows, early_sums, teacher_gain[None, :], align_weights)

    mixed, scale_rows, base = lax.optimization_barrier((mixed, scale_rows, base))

    cut = rows_here // 2
    up = along_tp(mixed, lambda t: (t + 2) % tp_count)
    down = along_tp(mixed, lambda t: (t - 2) % tp_count)
    far = jnp.concatenate(
        [
            along_tp(up[:cut], lambda t: (t + 2) % tp_count),
            along_tp(down[cut:], lambda t: (t - 2) % tp_count),
        ],
        axis=0,
    )
    parts = [mixed, up, down, far]
    near = len(parts)
    parts += [along_tp(part, lambda t: t ^ 1) for part in parts]
    shifts = jnp.array([0, -2, 2, 4], jnp.int32)
    order = jnp.concatenate([(tp_index + shifts) % tp_count, ((tp_index ^ 1) + shifts) % tp_count])

    target, sums = pl.pallas_call(
        project_body,
        out_shape=(
            pltpu.HBM((columns, rows_here), BF16),
            jax.ShapeDtypeStruct((tp_count, 8, LANES), F32),
        ),
        in_specs=[SMEM] + [VMEM] * near + [HBM] * (SIDE - near + 2),
        out_specs=[HBM, VMEM],
        scratch_shapes=[
            pltpu.VMEM((rows_here, columns), F32),
            pltpu.VMEM((columns, rows_here), BF16),
            pltpu.VMEM((columns, rows_here), F32),
            pltpu.VMEM((SIDE, columns, group), BF16),
            pltpu.VMEM((SIDE - near, rows_here, group), BF16),
            pltpu.SemaphoreType.DMA((2, SIDE)),
            pltpu.SemaphoreType.DMA((2,)),
        ],
        compiler_params=pltpu.CompilerParams(vmem_limit_bytes=26 << 20),
        name="project",
    )(
        order.astype(jnp.int32),
        *parts,
        pltpu.with_memory_space_constraint(all_map, pltpu.HBM),
        pltpu.with_memory_space_constraint(gained, pltpu.HBM),
    )

    sums = exchanged(sums, "tp")
    terms = pl.pallas_call(
        functools.partial(terms_body, width=student_width, count=seq_rows),
        out_shape=jax.ShapeDtypeStruct((seq_count, columns // LANES, LANES), F32),
        in_specs=[VMEM] * 5,
        out_specs=VMEM,
        name="terms",
    )(sums, scale_rows, base, target, student)
    gain_grad = exchanged(terms, "seq").sum(axis=0).reshape(columns)
    row_grad = pl.pallas_call(
        functools.partial(grad_body, width=student_width),
        out_shape=jax.ShapeDtypeStruct((rows_here, columns), BF16),
        in_specs=[VMEM] * 5,
        out_specs=VMEM,
        cost_estimate=pl.CostEstimate(flops=4 << 20, bytes_accessed=2 << 20, transcendentals=0),
        name="grad",
    )(sums, scale_rows, target, student, gain_row)
    return (row_grad, gain_grad)


def solution(mesh):
    placed = (
        P("seq", "tp"),
        P("tp"),
        P(),
        P("tp", "seq"),
        P("seq", "tp"),
        P("tp"),
        P("seq"),
        P("seq"),
        P("seq", None),
    )
    return jax.shard_map(
        shards, mesh=mesh, in_specs=placed, out_specs=(P("seq", "tp"), P("tp")), check_vma=False
    )
```

```python
import functools

import jax
import jax.numpy as jnp
from jax import lax
from jax.experimental import pallas as pl
from jax.experimental.pallas import tpu as pltpu
from jax.sharding import PartitionSpec as P


epsilon = 1e-06
LEFT = 128
RIGHT = 160
SIDE = 8
F32 = jnp.float32
BF16 = jnp.bfloat16
VMEM = pl.BlockSpec(memory_space=pltpu.VMEM)
SMEM = pl.BlockSpec(memory_space=pltpu.SMEM)
HBM = pl.BlockSpec(memory_space=pltpu.HBM)
LANES = 128


def exchanged(copies, axis):
    return lax.all_to_all(copies, axis, split_axis=0, concat_axis=0, tiled=True)


def sent_to_all(value, axis):
    return exchanged(jnp.broadcast_to(value, (lax.axis_size(axis), *value.shape)), axis)


def moved(value, place):
    pairs = []
    for y in range(SIDE):
        for z in range(SIDE):
            for t in range(SIDE):
                y2, z2, t2 = place(y, z, t)
                pairs.append(((y * SIDE + z) * SIDE + t, (y2 * SIDE + z2) * SIDE + t2))
    return lax.ppermute(value, ("seq", "tp"), pairs)


def along_tp(value, to):
    return lax.ppermute(value, "tp", [(t, to(t)) for t in range(SIDE)])


def column(row):
    return jnp.transpose(jnp.broadcast_to(row, (128, row.shape[1])))[:, :1]


def row(values):
    return jnp.transpose(jnp.broadcast_to(values, (values.shape[0], 128)))[:1, :]


def times(left, right):
    return lax.dot_general(left, right, (((1,), (1,)), ((), ())), preferred_element_type=F32)


def student_body(student_ref, gain_ref, turned_ref, gained_ref, sums_ref):
    turned = jnp.transpose(student_ref[...].astype(F32))
    turned_ref[...] = turned.astype(BF16)
    sums_ref[0:1, :] = jnp.sum(turned * turned, axis=0, keepdims=True)
    gained = turned * column(gain_ref[...])
    gained_ref[...] = gained
    sums_ref[1:2, :] = jnp.sum(gained * gained, axis=0, keepdims=True)


def mix_body(place_ref, rows_ref, sums_ref, gain_ref, weights_ref, out_ref, *, slots, width):
    blocks, block = place_ref.shape[1], weights_ref.shape[1]
    total = rows_ref.shape[0]
    sums = jnp.sum(sums_ref[...], axis=0)[:, :total]
    scale = lax.rsqrt(sums / width + epsilon)
    within = lax.broadcasted_iota(jnp.int32, (block, total), 0)
    spot = lax.broadcasted_iota(jnp.int32, (block, total), 1)
    gain = gain_ref[...]
    rows = rows_ref[...]
    for k in range(blocks):
        start, length, count = place_ref[0, k], place_ref[1, k], place_ref[2, k]
        place = within + start
        held = jnp.where(
            place < 0,
            place + (slots + LEFT),
            jnp.where(place < count, place, place - count + (slots + LEFT)),
        )
        chosen = jnp.where((spot == held) & (within < length), 1.0, 0.0).astype(BF16)
        weights = weights_ref[pl.ds(k * block, block), :]
        spread = jnp.dot(weights, chosen, preferred_element_type=F32)
        spread = (spread * scale).astype(BF16)
        mixed = jnp.dot(spread, rows, preferred_element_type=F32)
        out_ref[pl.ds(k * block, block), :] = (mixed * gain).astype(BF16)


def ready_body(sums_ref, student_ref, gain_ref, rows_ref, base_ref, *, width):
    count = student_ref.shape[1]
    total = jnp.sum(sums_ref[...], axis=0)
    at = total.shape[1] - 2 * count
    student_scale = lax.rsqrt(total[:, at : at + count] / width + epsilon)
    rows_ref[0:1, :] = student_scale
    rows_ref[1:2, :] = student_scale * total[:, at + count :]
    student_hat = student_ref[...].astype(F32) * student_scale
    base_ref[...] = row(jnp.sum(student_hat * student_hat, axis=1, keepdims=True)) * gain_ref[...]


def project_body(order_ref, *refs):
    parts, refs = refs[:SIDE], refs[SIDE:]
    map_ref, gained_in, target_out, sums_ref, rounded_ref, gained_ref, held, mixed, sem, side_sem = refs
    near = SIDE - mixed.shape[0]
    copies = [[] for _ in range(SIDE)]
    for i in range(SIDE):
        copies[i].append(pltpu.make_async_copy(map_ref.at[order_ref[i]], held.at[i], sem.at[0, i]))
        if i >= near:
            copies[i].append(pltpu.make_async_copy(parts[i], mixed.at[i - near], sem.at[1, i]))
        for copy in copies[i]:
            copy.start()
    take_gained = pltpu.make_async_copy(gained_in, gained_ref, side_sem.at[0])
    take_gained.start()
    for i in range(SIDE):
        for copy in copies[i]:
            copy.wait()
        part = times(parts[i][...] if i < near else mixed[i - near], held[i])
        total = part if i == 0 else total + part
    target = jnp.transpose(total)
    rounded_ref[...] = target.astype(BF16)
    send = pltpu.make_async_copy(rounded_ref, target_out, side_sem.at[1])
    send.start()
    take_gained.wait()
    sums_ref[:, 6:8, :] = jnp.zeros((SIDE, 2, LANES), F32)
    fill(sums_ref, 0, jnp.sum(target * target, axis=0, keepdims=True))
    fill(sums_ref, 3, jnp.sum(target * gained_ref[...], axis=0, keepdims=True))
    send.wait()


def fill(ref, at, values):
    for k in range(values.shape[1] // LANES):
        piece = values[:, k * LANES : (k + 1) * LANES]
        ref[:, at + k : at + k + 1, :] = jnp.broadcast_to(piece[None], (ref.shape[0], 1, LANES))


def late_sums(sums_ref, width):
    total = jnp.sum(sums_ref[...], axis=0)
    target_sums = jnp.concatenate([total[k : k + 1] for k in range(3)], axis=1)
    cross = jnp.concatenate([total[k : k + 1] for k in range(3, 6)], axis=1)
    return lax.rsqrt(target_sums / width + epsilon), cross


def terms_body(sums_ref, rows_ref, base_ref, target_ref, student_ref, terms_ref, *, width):
    target_scale, _ = late_sums(sums_ref, width)
    scale = target_scale * rows_ref[0:1, :]
    cross = target_ref[...].astype(F32) * student_ref[...].astype(F32)
    taken = row(jnp.sum(cross * scale, axis=1, keepdims=True))
    fill(terms_ref, 0, base_ref[...] - taken)


def grad_body(sums_ref, rows_ref, target_ref, student_ref, gain_ref, grad_ref, *, width):
    target_scale, cross = late_sums(sums_ref, width)
    scale = rows_ref[0:1, :]
    inner = scale * (rows_ref[1:2, :] - target_scale * cross) / width
    gain = column(gain_ref[...])
    student_hat = student_ref[...].astype(F32) * scale
    target_hat = target_ref[...].astype(F32) * target_scale
    grad = scale * ((student_hat * gain - target_hat) * gain - student_hat * inner)
    grad_ref[...] = jnp.transpose(grad).astype(BF16)


def shards(
    teacher_rows,
    teacher_gain,
    teacher_counts,
    projector,
    student_rows,
    student_gain,
    span_shift,
    span_len,
    align_weights,
):
    seq_count = lax.axis_size("seq")
    tp_count = lax.axis_size("tp")
    position = lax.axis_index("seq")
    tp_index = lax.axis_index("tp")
    slots, group = teacher_rows.shape
    teacher_width = group * tp_count
    rows_here, columns = student_rows.shape
    student_width = columns * tp_count
    blocks = span_shift.shape[0]
    seq_rows = rows_here * seq_count
    gain_row = student_gain[None, :]

    own_map = moved(projector.T, lambda y, z, t: (t, z, y))

    own_count = jnp.take(teacher_counts, position)
    before = jnp.take(teacher_counts, jnp.maximum(position - 1, 0))
    own_start = jnp.where(position % 2 == 0, position * rows_here, (position - 1) * rows_here + before)
    last_rows = lax.dynamic_slice_in_dim(teacher_rows, own_count - LEFT, LEFT, axis=0)
    left = lax.ppermute(last_rows, "seq", [(i, (i + 1) % seq_count) for i in range(seq_count)])
    right = lax.ppermute(
        teacher_rows[:RIGHT], "seq", [(i, (i - 1) % seq_count) for i in range(seq_count)]
    )

    student, gained, student_sums = pl.pallas_call(
        student_body,
        out_shape=(
            jax.ShapeDtypeStruct((columns, rows_here), BF16),
            jax.ShapeDtypeStruct((columns, rows_here), F32),
            jax.ShapeDtypeStruct((2, rows_here), F32),
        ),
        in_specs=[VMEM] * 2,
        out_specs=[VMEM] * 3,
        name="student",
    )(student_rows, gain_row)

    all_map = lax.all_gather(own_map, "seq", axis=0, tiled=True).reshape(SIDE, columns, group)

    rows = jnp.concatenate([teacher_rows, left, right], axis=0)
    square_sums = jnp.sum(jnp.square(rows.astype(F32)), axis=1)
    early_sums = jnp.concatenate([square_sums, student_sums.reshape(-1)])[None, :]
    early_sums = sent_to_all(early_sums, "tp")
    scale_rows, base = pl.pallas_call(
        functools.partial(ready_body, width=student_width),
        out_shape=(
            jax.ShapeDtypeStruct((2, rows_here), F32),
            jax.ShapeDtypeStruct((1, columns), F32),
        ),
        in_specs=[VMEM] * 3,
        out_specs=[VMEM] * 2,
        name="ready",
    )(early_sums, student, gain_row)
    block_ids = jnp.arange(blocks, dtype=jnp.int32)
    first = block_ids * own_count // blocks + span_shift
    first = jnp.clip(first, -own_start, seq_rows - span_len - own_start)
    place = jnp.stack([first, span_len, jnp.broadcast_to(own_count, (blocks,))]).astype(jnp.int32)
    mixed = pl.pallas_call(
        functools.partial(mix_body, slots=slots, width=teacher_width),
        out_shape=jax.ShapeDtypeStruct((rows_here, group), BF16),
        in_specs=[SMEM, VMEM, VMEM, VMEM, VMEM],
        out_specs=VMEM,
        name="mix",
    )(place, rows, early_sums, teacher_gain[None, :], align_weights)

    mixed, scale_rows, base = lax.optimization_barrier((mixed, scale_rows, base))

    cut = rows_here // 2
    up = along_tp(mixed, lambda t: (t + 2) % tp_count)
    down = along_tp(mixed, lambda t: (t - 2) % tp_count)
    far = jnp.concatenate(
        [
            along_tp(up[:cut], lambda t: (t + 2) % tp_count),
            along_tp(down[cut:], lambda t: (t - 2) % tp_count),
        ],
        axis=0,
    )
    parts = [mixed, up, down, far]
    near = len(parts)
    parts += [along_tp(part, lambda t: t ^ 1) for part in parts]
    shifts = jnp.array([0, -2, 2, 4], jnp.int32)
    order = jnp.concatenate([(tp_index + shifts) % tp_count, ((tp_index ^ 1) + shifts) % tp_count])

    target, sums = pl.pallas_call(
        project_body,
        out_shape=(
            pltpu.HBM((columns, rows_here), BF16),
            jax.ShapeDtypeStruct((tp_count, 8, LANES), F32),
        ),
        in_specs=[SMEM] + [VMEM] * near + [HBM] * (SIDE - near + 2),
        out_specs=[HBM, VMEM],
        scratch_shapes=[
            pltpu.VMEM((columns, rows_here), BF16),
            pltpu.VMEM((columns, rows_here), F32),
            pltpu.VMEM((SIDE, columns, group), BF16),
            pltpu.VMEM((SIDE - near, rows_here, group), BF16),
            pltpu.SemaphoreType.DMA((2, SIDE)),
            pltpu.SemaphoreType.DMA((2,)),
        ],
        compiler_params=pltpu.CompilerParams(vmem_limit_bytes=26 << 20),
        name="project",
    )(
        order.astype(jnp.int32),
        *parts,
        pltpu.with_memory_space_constraint(all_map, pltpu.HBM),
        pltpu.with_memory_space_constraint(gained, pltpu.HBM),
    )

    sums = exchanged(sums, "tp")
    terms = pl.pallas_call(
        functools.partial(terms_body, width=student_width),
        out_shape=jax.ShapeDtypeStruct((seq_count, columns // LANES, LANES), F32),
        in_specs=[VMEM] * 5,
        out_specs=VMEM,
        name="terms",
    )(sums, scale_rows, base, target, student)
    gain_grad = exchanged(terms, "seq").sum(axis=0).reshape(columns) / seq_rows
    row_grad = pl.pallas_call(
        functools.partial(grad_body, width=student_width),
        out_shape=jax.ShapeDtypeStruct((rows_here, columns), BF16),
        in_specs=[VMEM] * 5,
        out_specs=VMEM,
        cost_estimate=pl.CostEstimate(flops=4 << 20, bytes_accessed=2 << 20, transcendentals=0),
        name="grad",
    )(sums, scale_rows, target, student, gain_row)
    return (row_grad, gain_grad)


def solution(mesh):
    placed = (
        P("seq", "tp"),
        P("tp"),
        P(),
        P("tp", "seq"),
        P("seq", "tp"),
        P("tp"),
        P("seq"),
        P("seq"),
        P("seq", None),
    )
    return jax.shard_map(
        shards, mesh=mesh, in_specs=placed, out_specs=(P("seq", "tp"), P("tp")), check_vma=False
    )
```
